512 devices in a mesh: ex: 32 (over z, core), pb: 16 (over y, x).
Axes of the slice: x: 4, y: 4, z: 16, core: 2. Of those that a mesh axis runs over, the one named last changes fastest.
Arguments:
- train_sketch: bfloat16 [98304, 8192], P(('ex', 'pb')), may hold values from -6 to 6
- query_sketch: bfloat16 [768, 8192], P('pb'), may hold values from -0.0625 to 0.0625
- residual: float32 [98304], P(('ex', 'pb')), may hold values from 0.05 to 1
- example_source: int32 [98304], P(('ex', 'pb')), may hold values from 0 to 32767, as said below
- source_place: int32 [32768], replicated, may hold values from 0 to 32767, as said below
Outputs:
- source_scores: float32 [32768, 768], P(('ex', 'pb'))
The draws below stay inside these ranges and needn't reach their ends.
Inputs may be any that keep to these rules, and one draw needn't show every extreme that they name: source_place names each row 0 to 32767 once. `example_source`: of the 192 examples of one device, at most 12 have sources whose table row lies with any one owner (row // 1024); one owner receives exactly 12 from every device. Of them, at most 1 have table rows in any one share of that owner (row % 1024 // (1024 / 16)); in every draw some share of one owner receives exactly 1 from every device.
All inputs are finite; a program needn't handle non-finite values.
Results may differ from the reference program's by a relative error of at most 0.0029.
Values may be sent and summed in bfloat16 or wider, within the bound.
A program may use at most 64 MiB of HBM per device.

```python
import jax
import jax.numpy as jnp

K = 8192
Q = 768
ROWS = 192
SRC_DEV = 1024
CAP = 12
EXAMPLES = 98304
SOURCES = 32768
N_EX = 32
N_PB = 16


def swap_entry(table, value, position):
    found = jnp.argmax((table == value).astype(jnp.int32)).astype(jnp.int32)
    there = table[position]
    table = table.at[found].set(there)
    return table.at[position].set(value)


def joint_tables(key):
    base = jax.random.fold_in(key, 11)
    key_place, key_hot, key_perm, key_rows, key_slot = jax.random.split(base, 5)
    blocks = N_EX * N_PB
    share_width = SRC_DEV // N_PB
    hottest = jax.random.randint(key_hot, (), 0, N_EX).astype(jnp.int32)
    inverse = jax.random.permutation(key_place, SOURCES).astype(jnp.int32)
    inverse = swap_entry(inverse, jnp.int32(0), hottest * SRC_DEV)
    inverse = swap_entry(inverse, jnp.int32(SOURCES - 1), hottest * SRC_DEV + 2 * share_width - 1)
    placed = jnp.zeros((SOURCES,), jnp.int32).at[inverse].set(jnp.arange(SOURCES, dtype=jnp.int32))
    others = jax.vmap(lambda k: jax.random.permutation(k, N_EX - 1))(jax.random.split(key_perm, blocks)).astype(jnp.int32)
    column = jnp.arange(ROWS, dtype=jnp.int32)
    index_other = (column - CAP) % (N_EX - 1)
    picked = others[:, index_other]
    picked = jnp.where(picked >= hottest, picked + 1, picked)
    owner_id = jnp.where(column[None, :] < CAP, hottest, picked).astype(jnp.int32)
    rank_owner = jnp.where(column < CAP, column, (column - CAP) // (N_EX - 1)).astype(jnp.int32)
    share_no = (rank_owner % N_PB).astype(jnp.int32)
    within = jax.random.randint(key_slot, (blocks, ROWS), 0, share_width).astype(jnp.int32)
    block_no = jnp.arange(blocks, dtype=jnp.int32)[:, None]
    within = jnp.where((block_no == 0) & (column[None, :] < 2), column[None, :] * (share_width - 1), within).astype(jnp.int32)
    slot_id = (share_no[None, :] * share_width + within).astype(jnp.int32)
    orders = jax.vmap(lambda k: jax.random.permutation(k, ROWS))(jax.random.split(key_rows, blocks)).astype(jnp.int32)
    owner_id = jnp.take_along_axis(owner_id, orders, axis=1)
    slot_id = jnp.take_along_axis(slot_id, orders, axis=1)
    source_ids = inverse[owner_id * SRC_DEV + slot_id].reshape(-1)
    return (placed, source_ids)


def draw_source_place(key, part):
    return joint_tables(key)[0]


def draw_example_source(key, part):
    return joint_tables(key)[1]


def steps_of(rng, shape, cuts, low, top_value):
    factor_of = 1.0
    for dim, blocks in cuts:
        draws = jax.random.uniform(jax.random.fold_in(jax.random.fold_in(rng, 6), dim), (blocks,), jnp.float32, low / len(cuts), top_value / len(cuts))
        factor_of = factor_of * jnp.repeat(jnp.exp(draws), shape[dim] // blocks).reshape((-1,) + (1,) * (len(shape) - 1 - dim))
    return factor_of


def scatter_about(own_key, dims, spread, limit, shards=(), kind=jnp.bfloat16):
    drawn = jax.random.normal(own_key, dims, jnp.float32) * spread
    if len(shards) > 0:
        drawn = steps_of(own_key, dims, shards, -0.22, 0.18) * drawn
    return jnp.clip(drawn, min=-limit, max=limit).astype(kind)


def setup_inputs(seed: int = 0) -> dict:
    key_of = jax.random.split(jax.random.key(seed), 6)
    train_sketch = scatter_about(key_of[0], (EXAMPLES, K), 1.0, 6.0, ((0, 512),))
    query_sketch = scatter_about(key_of[1], (Q, K), K ** -0.5, 0.0625, ((0, 16),))
    residual = jnp.clip(0.05 + 0.95 * jax.random.uniform(key_of[2], (EXAMPLES,), jnp.float32) ** steps_of(key_of[2], (EXAMPLES,), ((0, 512),), -0.2, 0.2), 0.05, 1.0)
    example_source = draw_example_source(jax.random.fold_in(key_of[5], 71), 0)
    source_place = draw_source_place(jax.random.fold_in(key_of[5], 71), 0)
    return {"train_sketch": train_sketch, "query_sketch": query_sketch, "residual": residual, "example_source": example_source, "source_place": source_place}


def reference(train_sketch, query_sketch, residual, example_source, source_place):
    scores = jnp.dot(train_sketch, query_sketch.T, preferred_element_type=jnp.float32)
    weighted = (scores * residual[:, None]).astype(jnp.bfloat16)
    placed = source_place[example_source]
    return jax.ops.segment_sum(weighted.astype(jnp.float32), placed, num_segments=SOURCES)
```

```python
import jax
import jax.numpy as jnp
from jax import lax
from jax.experimental import pallas as pl
from jax.experimental.pallas import tpu as pltpu
from jax.sharding import PartitionSpec as P

MESH = pl.DeviceIdType.MESH
NZ, NC, NY, NX = 16, 2, 4, 4
NPB = NY * NX
ROWS, K = 192, 8192
HALF_K, QUARTER_K = K // 2, K // 4
QROWS, GROUPS, GROW = 24, 3, 8
LANES = NPB * GROW
CAP = 12
ZSLOT = 4 * CAP
PSLOT = 4 * NZ
SHARE = 64
QUERIES = 768
KSTEP = 1024
Z_ORDER = (8, 7, 9, 6, 10, 5, 11, 4, 12, 3, 13, 2, 14, 1, 15)
P_ORDER = (
    (2, 2), (1, 2), (2, 1), (3, 2), (2, 3), (1, 1), (3, 3), (1, 3), (3, 1),
    (0, 2), (2, 0), (0, 1), (1, 0), (0, 3), (3, 0),
)
F32, BF16, I32 = jnp.float32, jnp.bfloat16, jnp.int32
EV_B, EV_C, EV_D, EV_E, EV_F, EV_G = range(6)


def iota(shape, dim):
    return lax.broadcasted_iota(I32, shape, dim)


def mm(a, b, dims=((1,), (0,))):
    return lax.dot_general(a, b, (dims, ((), ())), preferred_element_type=F32)


def onehot(mask):
    return jnp.where(mask, 1.0, 0.0).astype(BF16)


def kernel(
    train, query, res, src, place, out,
    q_all, a_all, tbl, bundle, p1, rescol, score, zs, zr, p2, pe, pr, smat, accb, resb,
    local_sem, ag_recv, ag_send, z_recv, z_send, p_recv, p_send, d_recv, d_send,
):
    ex, pb = lax.axis_index("ex"), lax.axis_index("pb")
    z, c, y, x = ex // NC, ex % NC, pb // NX, pb % NX

    def dev(dz=0, dc=0, dy=0, dx=0):
        return (
            ((z + dz) % NZ) * NC + (c + dc) % NC,
            ((y + dy) % NY) * NX + (x + dx) % NX,
        )

    copy_tbl = pltpu.make_async_copy(place, tbl, local_sem.at[0])
    copy_q = [
        pltpu.make_async_copy(
            query.at[pl.ds(pl.multiple_of(c * QROWS + g * GROW, 8), GROW)],
            q_all.at[g, pb],
            local_sem.at[1 + g],
        )
        for g in range(GROUPS)
    ]
    copy_a = pltpu.make_async_copy(train, a_all.at[c], local_sem.at[4])
    copy_tbl.start()
    for cp in copy_q:
        cp.start()
    copy_a.start()

    barrier = pltpu.get_barrier_semaphore()
    greeted = (
        [dev(dc=1)]
        + [dev(dz=d) for d in range(1, NZ)]
        + [dev(dy=d // NX, dx=d % NX) for d in range(1, NPB)]
    )
    for there in greeted:
        pl.semaphore_signal(barrier, inc=1, device_id=there, device_id_type=MESH)

    copy_tbl.wait()
    ids = src[...]
    table = tbl[...]
    chosen = onehot(iota((256, ROWS), 0) == (ids >> 7))
    high = mm((table >> 7).astype(F32).astype(BF16), chosen, ((0,), (0,)))
    low = mm((table & 127).astype(F32).astype(BF16), chosen, ((0,), (0,)))
    lane = iota((128, ROWS), 0) == (ids & 127)
    placed = jnp.sum(jnp.where(lane, high * 128.0 + low, 0.0), axis=0, keepdims=True)
    placed = placed.astype(I32)
    owner, share, row = placed >> 10, (placed >> 6) & 15, placed & 63
    same = iota((32, ROWS), 0) == owner
    before = onehot(iota((ROWS, ROWS), 0) < iota((ROWS, ROWS), 1))
    rank = jnp.sum(jnp.where(same, mm(onehot(same), before), 0.0), axis=0, keepdims=True)
    core_of = owner & 1
    slot = ((owner >> 1) * ZSLOT + core_of * (2 * CAP) + c * CAP).astype(F32) + rank
    code = (share * 8 + (z % 2) * 4 + c * 2 + core_of + 1).astype(F32)
    row_code = (core_of * SHARE + row + 1).astype(F32)
    line = iota((8, ROWS), 0)
    packed = jnp.where(line == 0, slot, jnp.where(line == 1, code, row_code))
    bundle[c, :, 0:ROWS] = jnp.where(line == 3, res[...], packed)

    for cp in copy_q:
        cp.wait()
    pl.semaphore_wait(barrier, len(greeted))

    def remote(src_ref, dst_ref, send, recv, there):
        cp = pltpu.make_async_remote_copy(
            src_ref=src_ref, dst_ref=dst_ref, send_sem=send, recv_sem=recv,
            device_id=there, device_id_type=MESH,
        )
        cp.start()
        return cp

    pair_bundle = remote(bundle.at[c], bundle.at[c], d_send.at[0], d_recv.at[0], dev(dc=1))

    def source(path, df, ds):
        dy, dx = (ds, df) if path == 0 else (df, ds)
        return ((y + dy) % NY) * NX + (x + dx) % NX

    def pass_on(g, path, df, ds, part, first_axis, step, event):
        along_x = first_axis == (path == 0)
        there = dev(dx=step) if along_x else dev(dy=step)
        start, size = path * HALF_K, HALF_K
        if part is not None:
            start, size = start + part * QUARTER_K, QUARTER_K
        ref = q_all.at[g, source(path, df, ds), :, pl.ds(start, size)]
        remote(ref, ref, ag_send.at[g, path], ag_recv.at[g, path, event], there)

    def arrive(g, path, event, count):
        ref = q_all.at[g, pl.ds(0, count), :, pl.ds(0, HALF_K)]
        pltpu.make_async_copy(ref, ref, ag_recv.at[g, path, event]).wait()

    def both_ways(g, path, df, first_axis, event):
        for step in (1, -1):
            pass_on(g, path, df, 0, None, first_axis, step, event)

    def relay_second(g, path, df):
        pass_on(g, path, df, -1, 0, False, 1, EV_G)
        pass_on(g, path, df, 1, 1, False, -1, EV_G)

    def step_a(g):
        for path in (0, 1):
            both_ways(g, path, 0, True, EV_B)
        for path in (0, 1):
            both_ways(g, path, 0, False, EV_C)

    def step_b(g):
        for path in (0, 1):
            arrive(g, path, EV_B, 2)
            pass_on(g, path, -1, 0, 0, True, 1, EV_D)
            pass_on(g, path, 1, 0, 1, True, -1, EV_D)
            both_ways(g, path, -1, False, EV_E)
            both_ways(g, path, 1, False, EV_E)

    def step_c(g):
        for path in (0, 1):
            arrive(g, path, EV_C, 2)
            relay_second(g, path, 0)

    def step_d(g):
        for path in (0, 1):
            arrive(g, path, EV_D, 1)
            both_ways(g, path, 2, False, EV_F)

    def step_e(g):
        for path in (0, 1):
            arrive(g, path, EV_E, 4)
            relay_second(g, path, -1)
            relay_second(g, path, 1)

    def step_f(g):
        for path in (0, 1):
            arrive(g, path, EV_F, 2)
            relay_second(g, path, 2)

    def step_g(g):
        for path in (0, 1):
            arrive(g, path, EV_G, 4)

    def pack(t, part0, part1):
        rows = mm(p1[0], part0) + mm(p1[1], part1)
        zs[t] = rows.astype(BF16).reshape(NZ, ZSLOT, LANES)
        for d in Z_ORDER:
            remote(zs.at[t, (z + d) % NZ], zr.at[t, z], z_send.at[t], z_recv.at[t], dev(dz=d))
        zr[t, z] = zs[t, z]

    def z_arrive(t):
        ref = zr.at[t, pl.ds(0, NZ - 1)]
        pltpu.make_async_copy(ref, ref, z_recv.at[t]).wait()

    def spread(t):
        for pair in range(NZ // 2):
            rows = zr[t, 2 * pair : 2 * pair + 2].reshape(2 * ZSLOT, LANES)
            got = mm(p2[pair], rows).astype(BF16).reshape(NPB, 8, LANES)
            pe[t, :, 8 * pair : 8 * pair + 8, :] = got
        for dy, dx in P_ORDER:
            there = ((y + dy) % NY) * NX + (x + dx) % NX
            remote(pe.at[t, there], pr.at[t, pb], p_send.at[t], p_recv.at[t], dev(dy=dy, dx=dx))
        pr[t, pb] = pe[t, pb]

    def p_arrive(t):
        ref = pr.at[t, pl.ds(0, NPB - 1)]
        pltpu.make_async_copy(ref, ref, p_recv.at[t]).wait()

    def multiply(g):
        score[...] = jnp.zeros_like(score)

        def some(i, carry):
            k = pl.ds(pl.multiple_of(i * KSTEP, KSTEP), KSTEP)
            held = q_all[g, :, :, k].reshape(LANES, KSTEP)
            for s in (0, 1):
                score[s] += mm(a_all[s, :, k], held, ((1,), (1,)))
            return carry

        lax.fori_loop(0, K // KSTEP, some, 0)
        pack(g + 1, *[(score[s] * rescol[s]).astype(BF16) for s in (0, 1)])

    def finish(g):
        t = g + 1
        p_arrive(t)
        accb[g] = mm(smat[...], pr[t].reshape(NPB * PSLOT, LANES)).reshape(2, SHARE, LANES)
        return remote(accb.at[g, 1 - c], resb.at[g], d_send.at[2 + g], d_recv.at[2 + g], dev(dc=1))

    def place_columns(g, value, half):
        r, col = iota((LANES, QUERIES), 0), iota((LANES, QUERIES), 1)
        move = onehot(col == (r // 8) * 48 + r % 8 + g * GROW + half * QROWS)
        top = value.astype(BF16)
        rest = (value - top.astype(F32)).astype(BF16)
        return mm(top, move) + mm(rest, move)

    step_a(0)
    pair_a = remote(train, a_all.at[c], d_send.at[1], d_recv.at[1], dev(dc=1))
    step_b(0)
    pair_bundle.wait()
    eye = iota((ROWS, ROWS), 0) == iota((ROWS, ROWS), 1)

    def column(s, which):
        picked = jnp.where(eye, bundle[s, which : which + 1, 0:ROWS], 0.0)
        return jnp.sum(picked, axis=1, keepdims=True)

    notes = []
    for s in (0, 1):
        p1[s] = onehot(iota((NZ * ZSLOT, ROWS), 0) == bundle[s, 0:1, 0:ROWS].astype(I32))
        rescol[s] = jnp.broadcast_to(column(s, 3), (ROWS, LANES))
        left = iota((ROWS, LANES), 1) < 64
        notes.append(jnp.where(left, column(s, 1), column(s, 2)).astype(BF16))
    pack(0, *notes)
    step_c(0)
    step_d(0)
    step_a(1)
    step_e(0)
    step_b(1)
    step_f(0)
    step_c(1)
    step_d(1)
    z_arrive(0)
    for pair in range(NZ // 2):
        got = zr[0, 2 * pair : 2 * pair + 2].reshape(2 * ZSLOT, LANES).astype(F32)
        hit = (got[:, 0:1] - 1.0).astype(I32) == iota((2 * ZSLOT, 128), 1)
        p2[pair] = jnp.where(hit, 1.0, 0.0).T.astype(BF16)
    spread(0)
    step_g(0)
    copy_a.wait()
    pair_a.wait()
    multiply(0)
    step_a(2)
    step_e(1)
    step_b(2)
    step_f(1)
    step_c(2)
    step_d(2)
    p_arrive(0)
    got = pr[0].reshape(NPB * PSLOT, LANES).astype(F32)
    hit = (got[:, 64:65] - 1.0).astype(I32) == iota((NPB * PSLOT, 128), 1)
    smat[...] = jnp.where(hit, 1.0, 0.0).T.astype(BF16)
    step_g(1)
    multiply(1)
    z_arrive(1)
    spread(1)
    step_e(2)
    step_f(2)
    step_g(2)
    multiply(2)
    pair_acc = [finish(0)]
    z_arrive(2)
    spread(2)
    pair_acc.append(finish(1))
    total = place_columns(0, accb[0, c], c) + place_columns(1, accb[1, c], c)
    pair_acc[0].wait_recv()
    total += place_columns(0, resb[0], 1 - c)
    pair_acc[1].wait_recv()
    total += place_columns(1, resb[1], 1 - c)
    out[...] = total
    z_arrive(3)
    spread(3)
    pair_acc.append(finish(2))
    total = out[...] + place_columns(2, accb[2, c], c)
    pair_acc[2].wait_recv()
    out[...] = total + place_columns(2, resb[2], 1 - c)

    for cp in pair_acc:
        cp.wait_send()
    for g in range(GROUPS):
        for path in (0, 1):
            ref = q_all.at[g, pl.ds(0, 15), :, pl.ds(0, HALF_K)]
            pltpu.make_async_copy(ref, ref, ag_send.at[g, path]).wait()
    for t in range(GROUPS + 1):
        ref = zs.at[t, pl.ds(0, NZ - 1)]
        pltpu.make_async_copy(ref, ref, z_send.at[t]).wait()
        ref = pe.at[t, pl.ds(0, NPB - 1)]
        pltpu.make_async_copy(ref, ref, p_send.at[t]).wait()


def on_device(train_sketch, query_sketch, residual, example_source, source_place):
    anywhere = pl.BlockSpec(memory_space=pl.ANY)
    local = pl.BlockSpec(memory_space=pltpu.VMEM)
    t = GROUPS + 1
    dma = pltpu.SemaphoreType.DMA
    return pl.pallas_call(
        kernel,
        out_shape=jax.ShapeDtypeStruct((SHARE, QUERIES), F32),
        in_specs=[anywhere, anywhere, local, local, anywhere],
        out_specs=local,
        scratch_shapes=[
            pltpu.VMEM((GROUPS, NPB, GROW, K), BF16),
            pltpu.VMEM((NC, ROWS, K), BF16),
            pltpu.VMEM((256, 128), I32),
            pltpu.VMEM((NC, 8, 256), F32),
            pltpu.VMEM((NC, NZ * ZSLOT, ROWS), BF16),
            pltpu.VMEM((NC, ROWS, LANES), F32),
            pltpu.VMEM((NC, ROWS, LANES), F32),
            pltpu.VMEM((t, NZ, ZSLOT, LANES), BF16),
            pltpu.VMEM((t, NZ, ZSLOT, LANES), BF16),
            pltpu.VMEM((NZ // 2, 128, 2 * ZSLOT), BF16),
            pltpu.VMEM((t, NPB, PSLOT, LANES), BF16),
            pltpu.VMEM((t, NPB, PSLOT, LANES), BF16),
            pltpu.VMEM((128, NPB * PSLOT), BF16),
            pltpu.VMEM((GROUPS, 2, SHARE, LANES), F32),
            pltpu.VMEM((GROUPS, SHARE, LANES), F32),
            dma((5,)),
            dma((GROUPS, 2, 6)),
            dma((GROUPS, 2)),
            dma((t,)),
            dma((t,)),
            dma((t,)),
            dma((t,)),
            dma((2 + GROUPS,)),
            dma((2 + GROUPS,)),
        ],
        compiler_params=pltpu.CompilerParams(
            collective_id=1, has_side_effects=True, vmem_limit_bytes=48 * 1024 * 1024
        ),
        name="scores",
    )(
        train_sketch,
        query_sketch,
        residual.reshape(1, -1),
        example_source.reshape(1, -1),
        source_place.reshape(256, 128),
    )


def solution(mesh):
    return jax.shard_map(
        on_device,
        mesh=mesh,
        in_specs=(P(("ex", "pb"), None), P("pb", None), P(("ex", "pb")), P(("ex", "pb")), P()),
        out_specs=P(("ex", "pb"), None),
        check_vma=False,
    )
```

```python
import jax
import jax.numpy as jnp
from jax import lax
from jax.experimental import pallas as pl
from jax.experimental.pallas import tpu as pltpu
from jax.sharding import PartitionSpec as P

MESH = pl.DeviceIdType.MESH
NZ, NC, NY, NX = 16, 2, 4, 4
NPB = NY * NX
ROWS, K = 192, 8192
HALF_K, QUARTER_K = K // 2, K // 4
QROWS, GROUPS, GROW = 24, 3, 8
LANES = NPB * GROW
CAP = 12
ZSLOT = 4 * CAP
PSLOT = 4 * NZ
SHARE = 64
QUERIES = 768
KSTEP = 1024
Z_ORDER = (8, 7, 9, 6, 10, 5, 11, 4, 12, 3, 13, 2, 14, 1, 15)
P_ORDER = (
    (2, 2), (1, 2), (2, 1), (3, 2), (2, 3), (1, 1), (3, 3), (1, 3), (3, 1),
    (0, 2), (2, 0), (0, 1), (1, 0), (0, 3), (3, 0),
)
F32, BF16, I32 = jnp.float32, jnp.bfloat16, jnp.int32


def iota(shape, dim):
    return lax.broadcasted_iota(I32, shape, dim)


def mm(a, b, dims=((1,), (0,))):
    return lax.dot_general(a, b, (dims, ((), ())), preferred_element_type=F32)


def onehot(mask):
    return jnp.where(mask, 1.0, 0.0).astype(BF16)


def kernel(
    train, query, res, src, place, out,
    q_all, a_all, tbl, bundle, p1, rescol, score, zms, zmr, pms, pmr, pmf, zs, zr, p2, pe, pr, smat, accb, resb,
    z_up, z_down, local_sem, ag_recv, ag_send, zq_recv, zq_send, meta_recv, meta_send,
    z_recv, z_send, p_recv, p_send, d_recv, d_send,
):
    ex, pb = lax.axis_index("ex"), lax.axis_index("pb")
    z, c, y, x = ex // NC, ex % NC, pb // NX, pb % NX

    def dev(dz=0, dc=0, dy=0, dx=0):
        return (
            ((z + dz) % NZ) * NC + (c + dc) % NC,
            ((y + dy) % NY) * NX + (x + dx) % NX,
        )

    copy_tbl = pltpu.make_async_copy(place, tbl, local_sem.at[0])
    copy_q = [
        pltpu.make_async_copy(
            query.at[pl.ds(pl.multiple_of(c * QROWS + g * GROW, 8), GROW)],
            q_all.at[g, pb],
            local_sem.at[1 + g],
        )
        for g in range(GROUPS)
    ]
    copy_a = pltpu.make_async_copy(train, a_all.at[c], local_sem.at[4])
    copy_tbl.start()
    for cp in copy_q:
        cp.start()
    copy_a.start()

    barrier = pltpu.get_barrier_semaphore()
    greeted = (
        [dev(dc=1)]
        + [dev(dx=d) for d in (1, 2, 3)]
        + [dev(dy=d) for d in (1, 2, 3)]
        + [dev(dz=d) for d in (1, NZ - 1)]
    )
    for there in greeted:
        pl.semaphore_signal(barrier, inc=1, device_id=there, device_id_type=MESH)

    copy_tbl.wait()
    ids = src[...]
    table = tbl[...]
    chosen = onehot(iota((256, ROWS), 0) == (ids >> 7))
    high = mm((table >> 7).astype(F32).astype(BF16), chosen, ((0,), (0,)))
    low = mm((table & 127).astype(F32).astype(BF16), chosen, ((0,), (0,)))
    lane = iota((128, ROWS), 0) == (ids & 127)
    placed = jnp.sum(jnp.where(lane, high * 128.0 + low, 0.0), axis=0, keepdims=True)
    placed = placed.astype(I32)
    owner, share, row = placed >> 10, (placed >> 6) & 15, placed & 63
    same = iota((32, ROWS), 0) == owner
    before = onehot(iota((ROWS, ROWS), 0) < iota((ROWS, ROWS), 1))
    rank = jnp.sum(jnp.where(same, mm(onehot(same), before), 0.0), axis=0, keepdims=True)
    core_of = owner & 1
    spot = (core_of * (2 * CAP) + c * CAP).astype(F32) + rank
    slot = ((owner >> 1) * ZSLOT).astype(F32) + spot
    wide = ((owner >> 1) * 128 + (z % 2) * ZSLOT).astype(F32) + spot
    code = (share * 8 + (z % 2) * 4 + c * 2 + core_of + 1).astype(F32)
    row_code = (core_of * SHARE + row + 1).astype(F32)
    line = iota((8, ROWS), 0)
    packed = jnp.where(line == 0, slot, jnp.where(line == 1, code, row_code))
    packed = jnp.where(line == 3, res[...], packed)
    bundle[c, :, 0:ROWS] = jnp.where(line == 4, wide, packed)

    for cp in copy_q:
        cp.wait()
    pl.semaphore_wait(barrier, len(greeted))

    def remote(src_ref, dst_ref, send, recv, there):
        cp = pltpu.make_async_remote_copy(
            src_ref=src_ref, dst_ref=dst_ref, send_sem=send, recv_sem=recv,
            device_id=there, device_id_type=MESH,
        )
        cp.start()
        return cp

    pair_bundle = remote(bundle.at[c], bundle.at[c], d_send.at[0], d_recv.at[0], dev(dc=1))

    def source(path, df, ds):
        dy, dx = (ds, df) if path == 0 else (df, ds)
        return ((y + dy) % NY) * NX + (x + dx) % NX

    def columns(g, path):
        if g > 0:
            return pl.ds(path * HALF_K, HALF_K)
        return pl.ds(pl.multiple_of((z % 2) * HALF_K + path * QUARTER_K, 128), QUARTER_K)

    def pass_on(g, path, df, first_axis, event):
        ref = q_all.at[g, source(path, df, 0), :, columns(g, path)]
        for step in (2, 1, 3):
            there = dev(dx=step) if first_axis == (path == 0) else dev(dy=step)
            remote(ref, ref, ag_send.at[g, path], ag_recv.at[g, path, event], there)

    def arrive(g, path, event, count):
        ref = q_all.at[g, pl.ds(0, count), :, pl.ds(0, HALF_K if g > 0 else QUARTER_K)]
        pltpu.make_async_copy(ref, ref, ag_recv.at[g, path, event]).wait()

    def z_share(path, df, ds):
        ref = q_all.at[0, source(path, df, ds), :, columns(0, path)]
        remote(ref, ref, zq_send, zq_recv, dev(dz=1 if path == 0 else NZ - 1))

    def z_shared():
        ref = q_all.at[0, pl.ds(0, NPB - 1), :, pl.ds(0, HALF_K)]
        pltpu.make_async_copy(ref, ref, zq_recv).wait()

    def step_f(g):
        for path in (0, 1):
            pass_on(g, path, 0, True, 0)

    def step_s(g):
        for path in (0, 1):
            pass_on(g, path, 0, False, 1)

    def step_b(g):
        for path in (0, 1):
            arrive(g, path, 0, 3)
        for df in (2, 1, 3):
            for path in (0, 1):
                pass_on(g, path, df, False, 2)

    def step_g(g):
        for path in (0, 1):
            arrive(g, path, 1, 3)
            arrive(g, path, 2, 9)

    def z_tell():
        pl.semaphore_signal(z_up, inc=1, device_id=dev(dz=1), device_id_type=MESH)
        pl.semaphore_signal(z_down, inc=1, device_id=dev(dz=NZ - 1), device_id_type=MESH)

    def z_hear(rounds):
        for r in rounds:
            pl.semaphore_wait(z_up, 1)
            pl.semaphore_wait(z_down, 1)
            if r < NZ // 2 - 1:
                z_tell()

    def pack(t, part0, part1):
        rows = mm(p1[0], part0) + mm(p1[1], part1)
        zs[t] = rows.astype(BF16).reshape(NZ, ZSLOT, LANES)
        for d in Z_ORDER:
            remote(zs.at[t, (z + d) % NZ], zr.at[t, z], z_send.at[t], z_recv.at[t], dev(dz=d))
        zr[t, z] = zs[t, z]

    def z_arrive(t):
        ref = zr.at[t, pl.ds(0, NZ - 1)]
        pltpu.make_async_copy(ref, ref, z_recv.at[t]).wait()

    def spread(t):
        for pair in range(NZ // 2):
            rows = zr[t, 2 * pair : 2 * pair + 2].reshape(2 * ZSLOT, LANES)
            got = mm(p2[pair], rows).astype(BF16).reshape(NPB, 8, LANES)
            pe[t, :, 8 * pair : 8 * pair + 8, :] = got
        for dy, dx in P_ORDER:
            there = ((y + dy) % NY) * NX + (x + dx) % NX
            remote(pe.at[t, there], pr.at[t, pb], p_send.at[t], p_recv.at[t], dev(dy=dy, dx=dx))
        pr[t, pb] = pe[t, pb]

    def p_arrive(t):
        ref = pr.at[t, pl.ds(0, NPB - 1)]
        pltpu.make_async_copy(ref, ref, p_recv.at[t]).wait()

    def multiply(g):
        score[...] = jnp.zeros_like(score)

        def some(i, carry):
            k = pl.ds(pl.multiple_of(i * KSTEP, KSTEP), KSTEP)
            held = q_all[g, :, :, k].reshape(LANES, KSTEP)
            for s in (0, 1):
                score[s] += mm(a_all[s, :, k], held, ((1,), (1,)))
            return carry

        lax.fori_loop(0, K // KSTEP, some, 0)
        pack(g, *[(score[s] * rescol[s]).astype(BF16) for s in (0, 1)])

    def finish(g):
        p_arrive(g)
        accb[g] = mm(smat[...], pr[g].reshape(NPB * PSLOT, LANES)).reshape(2, SHARE, LANES)
        return remote(accb.at[g, 1 - c], resb.at[g], d_send.at[2 + g], d_recv.at[2 + g], dev(dc=1))

    def place_columns(g, value, half):
        r, col = iota((LANES, QUERIES), 0), iota((LANES, QUERIES), 1)
        move = onehot(col == (r // 8) * 48 + r % 8 + g * GROW + half * QROWS)
        top = value.astype(BF16)
        rest = (value - top.astype(F32)).astype(BF16)
        return mm(top, move) + mm(rest, move)

    def column(which, s):
        eye = iota((ROWS, ROWS), 0) == iota((ROWS, ROWS), 1)
        picked = jnp.where(eye, bundle[s, which : which + 1, 0:ROWS], 0.0)
        return jnp.sum(picked, axis=1, keepdims=True)

    def prepare():
        notes = jnp.zeros((8, NZ * 128), F32)
        for s in (0, 1):
            p1[s] = onehot(iota((NZ * ZSLOT, ROWS), 0) == bundle[s, 0:1, 0:ROWS].astype(I32))
            rescol[s] = jnp.broadcast_to(column(3, s), (ROWS, LANES))
            spots = onehot(iota((NZ * 128, ROWS), 0) == bundle[s, 4:5, 0:ROWS].astype(I32))
            values = jnp.where(iota((8, ROWS), 0) < 3, bundle[s, :, 0:ROWS], 0.0).astype(BF16)
            notes += mm(values, spots, ((1,), (1,)))
        for k in range(NZ):
            zms[k] = notes[:, k * 128 : k * 128 + 128].astype(BF16)

    def meta_z():
        for d in Z_ORDER:
            remote(zms.at[(z + d) % NZ], zmr.at[z], meta_send.at[0], meta_recv.at[0], dev(dz=d))
        zmr[z] = zms[z]

    def meta_plane():
        ref = zmr.at[pl.ds(0, NZ - 1)]
        pltpu.make_async_copy(ref, ref, meta_recv.at[0]).wait()
        for pair in range(NZ // 2):
            both = zmr[2 * pair].astype(F32) + zmr[2 * pair + 1].astype(F32)
            both = both[:, 0 : 2 * ZSLOT]
            p2[pair] = onehot(iota((128, 2 * ZSLOT), 0) == both[1:2].astype(I32) - 1)
            pmf[pair : pair + 1] = mm(both.astype(BF16), p2[pair], ((1,), (1,)))[2:3]
        pms[...] = pmf[...].astype(BF16)
        for dy, dx in P_ORDER:
            remote(pms, pmr.at[pb], meta_send.at[1], meta_recv.at[1], dev(dy=dy, dx=dx))
        pmr[pb] = pms[...]

    def meta_sum():
        ref = pmr.at[pl.ds(0, NPB - 1)]
        pltpu.make_async_copy(ref, ref, meta_recv.at[1]).wait()
        told = pmr[...].reshape(NPB * 8, 128)
        u = iota((NPB * PSLOT, 128), 0)
        spread_out = mm(onehot(u // 8 == iota((NPB * PSLOT, 128), 1)), told)
        mine = iota((NPB * PSLOT, 128), 1) == pb * 8 + u % 8
        value = jnp.sum(jnp.where(mine, spread_out, 0.0), axis=1, keepdims=True)
        hit = value.astype(I32) - 1 == iota((NPB * PSLOT, 128), 1)
        smat[...] = jnp.where(hit, 1.0, 0.0).T.astype(BF16)

    z_tell()
    step_f(0)
    step_s(0)
    step_f(1)
    pair_a = remote(train, a_all.at[c], d_send.at[1], d_recv.at[1], dev(dc=1))
    pair_bundle.wait()
    prepare()
    z_hear(range(0, 3))
    step_b(0)
    for df in (1, 2, 3):
        for path in (0, 1):
            z_share(path, df, 0)
    step_s(1)
    for path in (0, 1):
        arrive(0, path, 1, 3)
    for ds in (1, 2, 3):
        for path in (0, 1):
            z_share(path, 0, ds)
    z_hear(range(3, NZ // 2))
    meta_z()
    step_b(1)
    for path in (0, 1):
        arrive(0, path, 2, 9)
    for df in (1, 2, 3):
        for ds in (1, 2, 3):
            for path in (0, 1):
                z_share(path, df, ds)
    step_f(2)
    step_s(2)
    meta_plane()
    copy_a.wait()
    pair_a.wait()
    z_shared()
    multiply(0)
    step_b(2)
    step_g(1)
    multiply(1)
    meta_sum()
    z_arrive(0)
    spread(0)
    step_g(2)
    multiply(2)
    pair_acc = [finish(0)]
    z_arrive(1)
    spread(1)
    pair_acc.append(finish(1))
    total = place_columns(0, accb[0, c], c) + place_columns(1, accb[1, c], c)
    pair_acc[0].wait_recv()
    total += place_columns(0, resb[0], 1 - c)
    pair_acc[1].wait_recv()
    total += place_columns(1, resb[1], 1 - c)
    out[...] = total
    z_arrive(2)
    spread(2)
    pair_acc.append(finish(2))
    total = out[...] + place_columns(2, accb[2, c], c)
    pair_acc[2].wait_recv()
    out[...] = total + place_columns(2, resb[2], 1 - c)

    for cp in pair_acc:
        cp.wait_send()
    for g in range(GROUPS):
        for path in (0, 1):
            ref = q_all.at[g, pl.ds(0, 15), :, pl.ds(0, HALF_K if g > 0 else QUARTER_K)]
            pltpu.make_async_copy(ref, ref, ag_send.at[g, path]).wait()
        ref = zs.at[g, pl.ds(0, NZ - 1)]
        pltpu.make_async_copy(ref, ref, z_send.at[g]).wait()
        ref = pe.at[g, pl.ds(0, NPB - 1)]
        pltpu.make_async_copy(ref, ref, p_send.at[g]).wait()
    ref = q_all.at[0, pl.ds(0, NPB - 1), :, pl.ds(0, HALF_K)]
    pltpu.make_async_copy(ref, ref, zq_send).wait()
    ref = zms.at[pl.ds(0, NZ - 1)]
    pltpu.make_async_copy(ref, ref, meta_send.at[0]).wait()
    ref = pmr.at[pl.ds(0, NPB - 1)]
    pltpu.make_async_copy(ref, ref, meta_send.at[1]).wait()


def on_device(train_sketch, query_sketch, residual, example_source, source_place):
    anywhere = pl.BlockSpec(memory_space=pltpu.HBM)
    local = pl.BlockSpec(memory_space=pltpu.VMEM)
    t = GROUPS
    dma = pltpu.SemaphoreType.DMA
    return pl.pallas_call(
        kernel,
        out_shape=jax.ShapeDtypeStruct((SHARE, QUERIES), F32),
        in_specs=[anywhere, anywhere, local, local, anywhere],
        out_specs=local,
        scratch_shapes=[
            pltpu.VMEM((GROUPS, NPB, GROW, K), BF16),
            pltpu.VMEM((NC, ROWS, K), BF16),
            pltpu.VMEM((256, 128), I32),
            pltpu.VMEM((NC, 8, 256), F32),
            pltpu.VMEM((NC, NZ * ZSLOT, ROWS), BF16),
            pltpu.VMEM((NC, ROWS, LANES), F32),
            pltpu.VMEM((NC, ROWS, LANES), F32),
            pltpu.VMEM((NZ, 8, 128), BF16),
            pltpu.VMEM((NZ, 8, 128), BF16),
            pltpu.VMEM((8, 128), BF16),
            pltpu.VMEM((NPB, 8, 128), BF16),
            pltpu.VMEM((8, 128), F32),
            pltpu.VMEM((t, NZ, ZSLOT, LANES), BF16),
            pltpu.VMEM((t, NZ, ZSLOT, LANES), BF16),
            pltpu.VMEM((NZ // 2, 128, 2 * ZSLOT), BF16),
            pltpu.VMEM((t, NPB, PSLOT, LANES), BF16),
            pltpu.VMEM((t, NPB, PSLOT, LANES), BF16),
            pltpu.VMEM((128, NPB * PSLOT), BF16),
            pltpu.VMEM((GROUPS, 2, SHARE, LANES), F32),
            pltpu.VMEM((GROUPS, SHARE, LANES), F32),
            pltpu.SemaphoreType.REGULAR,
            pltpu.SemaphoreType.REGULAR,
            dma((5,)),
            dma((GROUPS, 2, 3)),
            dma((GROUPS, 2)),
            dma,
            dma,
            dma((2,)),
            dma((2,)),
            dma((t,)),
            dma((t,)),
            dma((t,)),
            dma((t,)),
            dma((2 + GROUPS,)),
            dma((2 + GROUPS,)),
        ],
        compiler_params=pltpu.CompilerParams(
            collective_id=1, has_side_effects=True, vmem_limit_bytes=48 * 1024 * 1024
        ),
        name="scores",
    )(
        train_sketch,
        query_sketch,
        residual.reshape(1, -1),
        example_source.reshape(1, -1),
        source_place.reshape(256, 128),
    )


def solution(mesh):
    return jax.shard_map(
        on_device,
        mesh=mesh,
        in_specs=(P(("ex", "pb"), None), P("pb", None), P(("ex", "pb")), P(("ex", "pb")), P()),
        out_specs=P(("ex", "pb"), None),
        check_vma=False,
    )
```

```python
import jax
import jax.numpy as jnp
from jax import lax
from jax.experimental import pallas as pl
from jax.experimental.pallas import tpu as pltpu
from jax.sharding import PartitionSpec as P

MESH = pl.DeviceIdType.MESH
NZ, NC, NY, NX = 16, 2, 4, 4
NPB = NY * NX
ROWS, K = 192, 8192
HALF_K, QUARTER_K = K // 2, K // 4
QROWS, GROUPS, GROW = 24, 3, 8
LANES = NPB * GROW
CAP = 12
ZSLOT = 4 * CAP
PSLOT = 4 * NZ
SHARE = 64
QUERIES = 768
KSTEP = 1024
PAIR_ORDER = (4, 3, 5, 2, 6, 1, 7, 0)
Z_ORDER = (8, 7, 9, 6, 10, 5, 11, 4, 12, 3, 13, 2, 14, 1, 15)
P_ORDER = (
    (2, 2), (1, 2), (2, 1), (3, 2), (2, 3), (1, 1), (3, 3), (1, 3), (3, 1),
    (0, 2), (2, 0), (0, 1), (1, 0), (0, 3), (3, 0),
)
F32, BF16, I32 = jnp.float32, jnp.bfloat16, jnp.int32


def iota(shape, dim):
    return lax.broadcasted_iota(I32, shape, dim)


def mm(a, b, dims=((1,), (0,))):
    return lax.dot_general(a, b, (dims, ((), ())), preferred_element_type=F32)


def onehot(mask):
    return jnp.where(mask, 1.0, 0.0).astype(BF16)


def kernel(
    train, query, res, src, place, out,
    q_all, a_all, tbl, bundle, p1, rescol, score, zms, zmr, pms, pmr, pmf, zs, zr, p2, pe, pr, smat, accb, resb,
    z_up, z_down, local_sem, ag_recv, ag_send, zq_recv, zq_send, meta_recv, meta_send,
    z_recv, z_send, p_recv, p_send, d_recv, d_send,
):
    ex, pb = lax.axis_index("ex"), lax.axis_index("pb")
    z, c, y, x = ex // NC, ex % NC, pb // NX, pb % NX

    def dev(dz=0, dc=0, dy=0, dx=0):
        return (
            ((z + dz) % NZ) * NC + (c + dc) % NC,
            ((y + dy) % NY) * NX + (x + dx) % NX,
        )

    copy_tbl = pltpu.make_async_copy(place, tbl, local_sem.at[0])
    copy_q = [
        pltpu.make_async_copy(
            query.at[pl.ds(pl.multiple_of(c * QROWS + g * GROW, 8), GROW)],
            q_all.at[g, pb],
            local_sem.at[1 + g],
        )
        for g in range(GROUPS)
    ]
    copy_a = pltpu.make_async_copy(train, a_all.at[c], local_sem.at[4])
    copy_tbl.start()
    for cp in copy_q:
        cp.start()
    copy_a.start()

    barrier = pltpu.get_barrier_semaphore()
    greeted = (
        [dev(dc=1)]
        + [dev(dx=d) for d in (1, 2, 3)]
        + [dev(dy=d) for d in (1, 2, 3)]
        + [dev(dz=d) for d in (1, 2, 3, 4, 12, 13, 14, 15)]
    )
    for there in greeted:
        pl.semaphore_signal(barrier, inc=1, device_id=there, device_id_type=MESH)

    for cp in copy_q:
        cp.wait()
    pl.semaphore_wait(barrier, len(greeted))

    def remote(src_ref, dst_ref, send, recv, there):
        cp = pltpu.make_async_remote_copy(
            src_ref=src_ref, dst_ref=dst_ref, send_sem=send, recv_sem=recv,
            device_id=there, device_id_type=MESH,
        )
        cp.start()
        return cp

    def meta_own():
        copy_tbl.wait()
        ids = src[...]
        table = tbl[...]
        chosen = onehot(iota((256, ROWS), 0) == (ids >> 7))
        high = mm((table >> 7).astype(F32).astype(BF16), chosen, ((0,), (0,)))
        low = mm((table & 127).astype(F32).astype(BF16), chosen, ((0,), (0,)))
        lane = iota((128, ROWS), 0) == (ids & 127)
        placed = jnp.sum(jnp.where(lane, high * 128.0 + low, 0.0), axis=0, keepdims=True)
        placed = placed.astype(I32)
        owner, share, row = placed >> 10, (placed >> 6) & 15, placed & 63
        same = iota((32, ROWS), 0) == owner
        before = onehot(iota((ROWS, ROWS), 0) < iota((ROWS, ROWS), 1))
        rank = jnp.sum(jnp.where(same, mm(onehot(same), before), 0.0), axis=0, keepdims=True)
        core_of = owner & 1
        spot = (core_of * (2 * CAP) + c * CAP).astype(F32) + rank
        slot = ((owner >> 1) * ZSLOT).astype(F32) + spot
        wide = ((owner >> 1) * 128 + (z % 2) * ZSLOT).astype(F32) + spot
        code = (share * 8 + (z % 2) * 4 + c * 2 + core_of + 1).astype(F32)
        row_code = (core_of * SHARE + row + 1).astype(F32)
        line = iota((8, ROWS), 0)
        packed = jnp.where(line == 0, slot, jnp.where(line == 1, code, row_code))
        packed = jnp.where(line == 3, res[...], packed)
        bundle[c, :, 0:ROWS] = jnp.where(line == 4, wide, packed)

    def source(path, df, ds):
        dy, dx = (ds, df) if path == 0 else (df, ds)
        return ((y + dy) % NY) * NX + (x + dx) % NX

    def columns(g, path, part=0):
        if g == 1:
            return pl.ds(path * HALF_K, HALF_K)
        start = path * HALF_K + part * QUARTER_K
        if g == 0:
            start = pl.multiple_of((z % 2) * HALF_K + path * QUARTER_K, 128)
        return pl.ds(start, QUARTER_K)

    def parts(g):
        return (0, 1) if g == 2 else (0,)

    def pass_on(g, path, df, first_axis, event, part=0):
        ref = q_all.at[g, source(path, df, 0), :, columns(g, path, part)]
        for step in (2, 1, 3):
            there = dev(dx=step) if first_axis == (path == 0) else dev(dy=step)
            arrived = ag_recv.at[g, path, event, part]
            remote(ref, ref, ag_send.at[g, path, part], arrived, there)

    def arrive(g, path, event, count, part=0):
        ref = q_all.at[g, pl.ds(0, count), :, pl.ds(0, HALF_K if g == 1 else QUARTER_K)]
        pltpu.make_async_copy(ref, ref, ag_recv.at[g, path, event, part]).wait()

    def z_share(path, df, ds):
        ref = q_all.at[0, source(path, df, ds), :, columns(0, path)]
        remote(ref, ref, zq_send, zq_recv, dev(dz=1 if path == 0 else NZ - 1))

    def z_shared():
        ref = q_all.at[0, pl.ds(0, NPB - 1), :, pl.ds(0, HALF_K)]
        pltpu.make_async_copy(ref, ref, zq_recv).wait()

    def step_f(g):
        for part in parts(g):
            for path in (0, 1):
                pass_on(g, path, 0, True, 0, part)

    def step_s(g):
        for part in parts(g):
            for path in (0, 1):
                pass_on(g, path, 0, False, 1, part)

    def step_b(g):
        for part in parts(g):
            for path in (0, 1):
                arrive(g, path, 0, 3, part)
            for df in (2, 1, 3):
                for path in (0, 1):
                    pass_on(g, path, df, False, 2, part)

    def step_g(g, part=0):
        for path in (0, 1):
            arrive(g, path, 1, 3, part)
            arrive(g, path, 2, 9, part)

    def z_tell():
        pl.semaphore_signal(z_up, inc=1, device_id=dev(dz=4), device_id_type=MESH)
        pl.semaphore_signal(z_down, inc=1, device_id=dev(dz=NZ - 4), device_id_type=MESH)

    def z_hear():
        pl.semaphore_wait(z_up, 1)
        pl.semaphore_wait(z_down, 1)

    def send_z(t):
        for d in Z_ORDER:
            half = ((z // 2 - ((z + d) % NZ) // 2 + 14) % 8) // 4
            remote(
                zs.at[t, (z + d) % NZ], zr.at[t, z], z_send.at[t], z_recv.at[t, half], dev(dz=d)
            )
        zr[t, z] = zs[t, z]

    def pack(t, part0, part1):
        rows = mm(p1[0], part0) + mm(p1[1], part1)
        zs[t] = rows.astype(BF16).reshape(NZ, ZSLOT, LANES)
        send_z(t)

    def z_arrive(t, half):
        ref = zr.at[t, pl.ds(0, NZ // 2 - half)]
        pltpu.make_async_copy(ref, ref, z_recv.at[t, half]).wait()

    def pair_at(o):
        return (z // 2 + PAIR_ORDER[o]) % (NZ // 2)

    def spread(t, half):
        for o in range(4 * half, 4 * half + 4):
            rows = zr[t, pl.ds(2 * pair_at(o), 2)].reshape(2 * ZSLOT, LANES)
            got = mm(p2[o], rows).astype(BF16).reshape(NPB, 8, LANES)
            pe[t, :, 8 * o : 8 * o + 8, :] = got
        rows = pl.ds(32 * half, 32)
        for dy, dx in P_ORDER:
            there = ((y + dy) % NY) * NX + (x + dx) % NX
            remote(
                pe.at[t, there, rows], pr.at[t, pb, rows],
                p_send.at[t, half], p_recv.at[t, half], dev(dy=dy, dx=dx),
            )
        pr[t, pb, rows] = pe[t, pb, rows]

    def p_arrive(t):
        for half in (0, 1):
            ref = pr.at[t, pl.ds(0, NPB - 1), pl.ds(0, 32)]
            pltpu.make_async_copy(ref, ref, p_recv.at[t, half]).wait()

    def multiply(g, start, size, first=False):
        if first:
            score[...] = jnp.zeros_like(score)

        def some(i, carry):
            k = pl.ds(pl.multiple_of(start + i * KSTEP, KSTEP), KSTEP)
            held = q_all[g, :, :, k].reshape(LANES, KSTEP)
            for s in (0, 1):
                score[s] += mm(a_all[s, :, k], held, ((1,), (1,)))
            return carry

        lax.fori_loop(0, size // KSTEP, some, 0)

    def weigh(g):
        pack(g, *[(score[s] * rescol[s]).astype(BF16) for s in (0, 1)])

    def finish(g):
        p_arrive(g)
        accb[g] = mm(smat[...], pr[g].reshape(NPB * PSLOT, LANES)).reshape(2, SHARE, LANES)
        return remote(accb.at[g, 1 - c], resb.at[g], d_send.at[2 + g], d_recv.at[2 + g], dev(dc=1))

    def place_columns(g, value, half):
        r, col = iota((LANES, QUERIES), 0), iota((LANES, QUERIES), 1)
        move = onehot(col == (r // 8) * 48 + r % 8 + g * GROW + half * QROWS)
        top = value.astype(BF16)
        rest = (value - top.astype(F32)).astype(BF16)
        return mm(top, move) + mm(rest, move)

    def column(which, s):
        eye = iota((ROWS, ROWS), 0) == iota((ROWS, ROWS), 1)
        picked = jnp.where(eye, bundle[s, which : which + 1, 0:ROWS], 0.0)
        return jnp.sum(picked, axis=1, keepdims=True)

    def prepare():
        notes = jnp.zeros((8, NZ * 128), F32)
        for s in (0, 1):
            p1[s] = onehot(iota((NZ * ZSLOT, ROWS), 0) == bundle[s, 0:1, 0:ROWS].astype(I32))
            rescol[s] = jnp.broadcast_to(column(3, s), (ROWS, LANES))
            spots = onehot(iota((NZ * 128, ROWS), 0) == bundle[s, 4:5, 0:ROWS].astype(I32))
            values = jnp.where(iota((8, ROWS), 0) < 3, bundle[s, :, 0:ROWS], 0.0).astype(BF16)
            notes += mm(values, spots, ((1,), (1,)))
        for k in range(NZ):
            zms[k] = notes[:, k * 128 : k * 128 + 128].astype(BF16)

    def meta_z():
        for d in Z_ORDER:
            remote(zms.at[(z + d) % NZ], zmr.at[z], meta_send.at[0], meta_recv.at[0], dev(dz=d))
        zmr[z] = zms[z]

    def meta_plane():
        ref = zmr.at[pl.ds(0, NZ - 1)]
        pltpu.make_async_copy(ref, ref, meta_recv.at[0]).wait()
        for o in range(NZ // 2):
            both = zmr[2 * pair_at(o)].astype(F32) + zmr[2 * pair_at(o) + 1].astype(F32)
            both = both[:, 0 : 2 * ZSLOT]
            p2[o] = onehot(iota((128, 2 * ZSLOT), 0) == both[1:2].astype(I32) - 1)
            pmf[o : o + 1] = mm(both.astype(BF16), p2[o], ((1,), (1,)))[2:3]
        pms[...] = pmf[...].astype(BF16)
        for dy, dx in P_ORDER:
            remote(pms, pmr.at[pb], meta_send.at[1], meta_recv.at[1], dev(dy=dy, dx=dx))
        pmr[pb] = pms[...]

    def meta_sum():
        ref = pmr.at[pl.ds(0, NPB - 1)]
        pltpu.make_async_copy(ref, ref, meta_recv.at[1]).wait()
        told = pmr[...].reshape(NPB * 8, 128)
        u = iota((NPB * PSLOT, 128), 0)
        spread_out = mm(onehot(u // 8 == iota((NPB * PSLOT, 128), 1)), told)
        mine = iota((NPB * PSLOT, 128), 1) == pb * 8 + u % 8
        value = jnp.sum(jnp.where(mine, spread_out, 0.0), axis=1, keepdims=True)
        hit = value.astype(I32) - 1 == iota((NPB * PSLOT, 128), 1)
        smat[...] = jnp.where(hit, 1.0, 0.0).T.astype(BF16)

    step_f(0)
    step_s(0)
    z_tell()
    step_f(1)
    pair_a = remote(train, a_all.at[c], d_send.at[1], d_recv.at[1], dev(dc=1))
    meta_own()
    pair_bundle = remote(bundle.at[c], bundle.at[c], d_send.at[0], d_recv.at[0], dev(dc=1))
    step_b(0)
    for df in (1, 2, 3):
        for path in (0, 1):
            z_share(path, df, 0)
    step_s(1)
    step_f(2)
    pair_bundle.wait()
    prepare()
    z_hear()
    meta_z()
    for path in (0, 1):
        arrive(0, path, 1, 3)
    for ds in (1, 2, 3):
        for path in (0, 1):
            z_share(path, 0, ds)
    for path in (0, 1):
        arrive(0, path, 2, 9)
    for df in (1, 2, 3):
        for ds in (1, 2, 3):
            for path in (0, 1):
                z_share(path, df, ds)
    step_b(1)
    step_s(2)
    copy_a.wait()
    pair_a.wait()
    own_half = (z % 2) * HALF_K
    multiply(0, own_half, HALF_K, True)
    meta_plane()
    z_shared()
    multiply(0, HALF_K - own_half, HALF_K)
    weigh(0)
    step_b(2)
    step_g(1)
    multiply(1, 0, K, True)
    weigh(1)
    meta_sum()
    for half in (0, 1):
        z_arrive(0, half)
        spread(0, half)
    for part in (0, 1):
        step_g(2, part)
        for path in (0, 1):
            multiply(2, path * HALF_K + part * QUARTER_K, QUARTER_K, part + path == 0)
    weigh(2)
    pair_acc = [finish(0)]
    for half in (0, 1):
        z_arrive(1, half)
        spread(1, half)
    pair_acc.append(finish(1))
    total = place_columns(0, accb[0, c], c) + place_columns(1, accb[1, c], c)
    pair_acc[0].wait_recv()
    total += place_columns(0, resb[0], 1 - c)
    pair_acc[1].wait_recv()
    total += place_columns(1, resb[1], 1 - c)
    out[...] = total
    for half in (0, 1):
        z_arrive(2, half)
        spread(2, half)
    pair_acc.append(finish(2))
    total = out[...] + place_columns(2, accb[2, c], c)
    pair_acc[2].wait_recv()
    out[...] = total + place_columns(2, resb[2], 1 - c)

    for cp in pair_acc:
        cp.wait_send()
    for g in range(GROUPS):
        for path in (0, 1):
            for part in parts(g):
                ref = q_all.at[g, pl.ds(0, 15), :, pl.ds(0, HALF_K if g == 1 else QUARTER_K)]
                pltpu.make_async_copy(ref, ref, ag_send.at[g, path, part]).wait()
        ref = zs.at[g, pl.ds(0, NZ - 1)]
        pltpu.make_async_copy(ref, ref, z_send.at[g]).wait()
        for half in (0, 1):
            ref = pe.at[g, pl.ds(0, NPB - 1), pl.ds(0, 32)]
            pltpu.make_async_copy(ref, ref, p_send.at[g, half]).wait()
    ref = q_all.at[0, pl.ds(0, NPB - 1), :, pl.ds(0, HALF_K)]
    pltpu.make_async_copy(ref, ref, zq_send).wait()
    ref = zms.at[pl.ds(0, NZ - 1)]
    pltpu.make_async_copy(ref, ref, meta_send.at[0]).wait()
    ref = pmr.at[pl.ds(0, NPB - 1)]
    pltpu.make_async_copy(ref, ref, meta_send.at[1]).wait()


def on_device(train_sketch, query_sketch, residual, example_source, source_place):
    anywhere = pl.BlockSpec(memory_space=pltpu.HBM)
    local = pl.BlockSpec(memory_space=pltpu.VMEM)
    t = GROUPS
    dma = pltpu.SemaphoreType.DMA
    return pl.pallas_call(
        kernel,
        out_shape=jax.ShapeDtypeStruct((SHARE, QUERIES), F32),
        in_specs=[anywhere, anywhere, local, local, anywhere],
        out_specs=local,
        scratch_shapes=[
            pltpu.VMEM((GROUPS, NPB, GROW, K), BF16),
            pltpu.VMEM((NC, ROWS, K), BF16),
            pltpu.VMEM((256, 128), I32),
            pltpu.VMEM((NC, 8, 256), F32),
            pltpu.VMEM((NC, NZ * ZSLOT, ROWS), BF16),
            pltpu.VMEM((NC, ROWS, LANES), F32),
            pltpu.VMEM((NC, ROWS, LANES), F32),
            pltpu.VMEM((NZ, 8, 128), BF16),
            pltpu.VMEM((NZ, 8, 128), BF16),
            pltpu.VMEM((8, 128), BF16),
            pltpu.VMEM((NPB, 8, 128), BF16),
            pltpu.VMEM((8, 128), F32),
            pltpu.VMEM((t, NZ, ZSLOT, LANES), BF16),
            pltpu.VMEM((t, NZ, ZSLOT, LANES), BF16),
            pltpu.VMEM((NZ // 2, 128, 2 * ZSLOT), BF16),
            pltpu.VMEM((t, NPB, PSLOT, LANES), BF16),
            pltpu.VMEM((t, NPB, PSLOT, LANES), BF16),
            pltpu.VMEM((128, NPB * PSLOT), BF16),
            pltpu.VMEM((GROUPS, 2, SHARE, LANES), F32),
            pltpu.VMEM((GROUPS, SHARE, LANES), F32),
            pltpu.SemaphoreType.REGULAR,
            pltpu.SemaphoreType.REGULAR,
            dma((5,)),
            dma((GROUPS, 2, 3, 2)),
            dma((GROUPS, 2, 2)),
            dma,
            dma,
            dma((2,)),
            dma((2,)),
            dma((t, 2)),
            dma((t,)),
            dma((t, 2)),
            dma((t, 2)),
            dma((2 + GROUPS,)),
            dma((2 + GROUPS,)),
        ],
        compiler_params=pltpu.CompilerParams(
            collective_id=1, has_side_effects=True
        ),
        name="scores",
    )(
        train_sketch,
        query_sketch,
        residual.reshape(1, -1),
        example_source.reshape(1, -1),
        source_place.reshape(256, 128),
    )


def solution(mesh):
    return jax.shard_map(
        on_device,
        mesh=mesh,
        in_specs=(P(("ex", "pb"), None), P("pb", None), P(("ex", "pb")), P(("ex", "pb")), P()),
        out_specs=P(("ex", "pb"), None),
        check_vma=False,
    )
```
